32 devices in a mesh: row: 4 (over z), col: 2 (over x), pole: 4 (over y, core).
Axes of the slice: x: 2, y: 2, z: 4, core: 2. Of those that a mesh axis runs over, the one named last changes fastest.
Arguments:
- window: bfloat16 [4, 8192, 8192], P('pole', 'col', 'row'), may hold values from -6 to 6
- panels: bfloat16 [4, 2, 8192, 256], P('pole', 'col', 'row'), may hold values from -0.0625 to 0.0625
- row_map: int32 [3, 8192], P(None, 'row'), may hold values from 0 to 8191, as said below
- panel_root: int32 [4, 3], P('pole'), may hold values from 0 to 1
- upper_blocks: bfloat16 [4, 3, 256, 256], P('pole', None, 'row'), may hold values from -0.375 to 0.375
- diag_inverse: float32 [4, 3, 256, 256], P('pole', None, 'row'), may hold values from -6 to 6
- weights: float32 [4], replicated, may hold values from 0.25 to 1
- pole_order: int32 [4], P('pole'), may hold values from 0 to 3, each once
Outputs:
- inv_columns: float32 [3, 2, 4096, 256], P(None, 'col', ('row', 'pole'))
- inv_diag: float32 [3, 256, 256], P(None, ('row', 'pole'))
The draws below stay inside these ranges and needn't reach their ends.
Inputs may be any that keep to these rules, and one draw needn't show every extreme that they name: row_map[k] permutes the positions inside each aligned group of 1024 consecutive positions. `pole_order`: each of the 4 poles appears once.
All inputs are finite; a program needn't handle non-finite values.
Results may differ from the reference program's by a relative error of at most 0.0003.
Values may be sent and summed in bfloat16 or wider, within the bound.
A program may use at most 128 MiB of HBM per device.

```python
import jax
import jax.numpy as jnp
from jax import lax

W = 8192
B = 256
NS = 3
NP = 4
NE = 3
GROUP = 1024
N_ROW = 4
N_COL = 2


def draw_row_map(key, part):
    blocks = NS * (W // GROUP)
    group_keys = jax.random.split(key, blocks)
    shuffled = jax.vmap(lambda one_key: jax.random.permutation(one_key, GROUP))(group_keys)
    offsets = jnp.arange(blocks) % (W // GROUP) * GROUP
    return (shuffled + offsets[:, None]).reshape(NS, W).astype(jnp.int32)


def set_ends(values, own_key, low, high):
    longest = values.shape.index(max(values.shape))
    spots = []
    for shift in (0, 1):
        where = [jax.random.randint(jax.random.fold_in(own_key, axis), (), 0, length) for axis, length in enumerate(values.shape)]
        where[longest] = (where[longest] + shift) % values.shape[longest]
        spots.append(tuple(where))
    return values.at[spots[0]].set(low).at[spots[1]].set(high)


def levels(stream_key, shape, cuts, least, largest):
    def one(axis_at, blocks):
        heights = jax.random.uniform(jax.random.fold_in(jax.random.fold_in(stream_key, 6), axis_at), (blocks,), jnp.float32, least / len(cuts), largest / len(cuts))
        return jnp.repeat(jnp.exp(heights), shape[axis_at] // blocks).reshape((-1,) + (1,) * (len(shape) - axis_at - 1))

    level = one(*cuts[0])
    for cut in cuts[1:]:
        level = level * one(*cut)
    return level


def noise(rng, extent, scale, bound, pieces=(), dtype=jnp.bfloat16):
    result = scale * jax.random.normal(rng, extent, jnp.float32)
    if pieces:
        result = result * levels(rng, extent, pieces, -0.22, 0.18)
    return jnp.clip(result, -bound, bound).astype(dtype)


def setup_inputs(seed: int = 0) -> dict:
    arg_keys = jax.random.split(jax.random.key(seed), 9)
    window = noise(arg_keys[0], (NP, W, W), 1.0, 6.0, ((0, 4), (1, 2), (2, 4)))
    panels = noise(arg_keys[1], (NP, N_COL, W, B), W ** -0.5, 0.0625, ((0, 4), (1, 2), (2, 4)))
    row_map = draw_row_map(jax.random.fold_in(arg_keys[8], 71), 0)
    panel_root = set_ends(jax.random.randint(arg_keys[3], (NP, NS), 0, N_COL), jax.random.fold_in(arg_keys[3], 1), 0, N_COL - 1).astype(jnp.int32)
    upper_blocks = noise(arg_keys[4], (NP, NE, B, B), B ** -0.5, 0.375, ((0, 4), (2, 4)))
    diag_inverse = noise(arg_keys[5], (NP, NS, B, B), 1.0, 6.0, ((0, 4), (2, 4)), jnp.float32)
    weights = jnp.clip(jax.random.uniform(arg_keys[6], (NP,), jnp.float32, 0.25, 1.0), 0.25, 1.0)
    pole_order = jax.random.permutation(arg_keys[7], NP).astype(jnp.int32)
    return {"window": window, "panels": panels, "row_map": row_map, "panel_root": panel_root, "upper_blocks": upper_blocks, "diag_inverse": diag_inverse, "weights": weights, "pole_order": pole_order}


def precise(left, right):
    return jnp.dot(left, right, precision=lax.Precision.HIGHEST, preferred_element_type=jnp.float32)


def pair_index(current, earlier):
    return current * (current - 1) // 2 + earlier


def inverse_block(diagonals, crossed, first, second):
    if first == second:
        return diagonals[first]
    if first < second:
        return crossed[(first, second)]
    return crossed[(second, first)].T


def natural_order(aligned):
    group_rows = W // (N_ROW * N_COL)
    width = aligned.shape[-1]
    return aligned.reshape(N_ROW, N_COL, group_rows, width).transpose(1, 0, 2, 3).reshape(W, width)


def reference(window, panels, row_map, panel_root, upper_blocks, diag_inverse, weights, pole_order):
    def one_pole(pole_index):
        window_block = window[pole_index]
        slot_panels = panels[pole_index]
        factors = upper_blocks[pole_index].astype(jnp.float32)
        inverses = diag_inverse[pole_index]
        pole_roots = lax.dynamic_index_in_dim(panel_root, pole_index, 0, keepdims=False)
        columns = []
        diagonals = []
        crossed = {}
        for current in range(NS):
            panel_slab = lax.dynamic_index_in_dim(slot_panels, pole_roots[current], 0, keepdims=False)
            aligned = jnp.take(panel_slab, row_map[current], axis=0)
            own_rows = natural_order(aligned).astype(jnp.float32)
            y_window = jnp.dot(window_block, aligned, preferred_element_type=jnp.float32)
            for earlier in range(current):
                y_window = y_window + precise(columns[earlier], factors[pair_index(current, earlier)])
            y_blocks = []
            for earlier in range(current):
                block_sum = precise(columns[earlier].T, own_rows)
                for other_node in range(current):
                    block_sum = block_sum + precise(inverse_block(diagonals, crossed, earlier, other_node), factors[pair_index(current, other_node)])
                y_blocks.append(block_sum)
            diagonal = inverses[current] + precise(own_rows.T, y_window)
            for earlier in range(current):
                diagonal = diagonal + precise(factors[pair_index(current, earlier)].T, y_blocks[earlier])
                crossed[(earlier, current)] = -y_blocks[earlier]
            columns.append(-y_window)
            diagonals.append(diagonal)
        return jnp.stack(columns), jnp.stack(diagonals)

    all_columns, all_diagonals = lax.map(one_pole, jnp.arange(NP))
    pole_weights = jnp.take(weights, pole_order)
    inv_columns = jnp.einsum("p,pkwb->kwb", pole_weights, all_columns).reshape(NS, N_COL, W // N_COL, B)
    inv_diag = jnp.einsum("p,pkab->kab", pole_weights, all_diagonals)
    return inv_columns, inv_diag
```

```python
import jax
import jax.numpy as jnp
from jax import lax
from jax.sharding import PartitionSpec as P

NS = 3
CHUNKS = 2


def precise(left, right):
    return jnp.dot(left, right, precision=lax.Precision.HIGHEST, preferred_element_type=jnp.float32)


def pair_index(current, earlier):
    return current * (current - 1) // 2 + earlier


def split(value):
    high = lax.reduce_precision(value, 8, 7)
    return high.astype(jnp.bfloat16), (value - high).astype(jnp.bfloat16)


def times_factor(halves, factor):
    high, low = halves
    return jnp.dot(high, factor, preferred_element_type=jnp.float32) + jnp.dot(
        low, factor, preferred_element_type=jnp.float32
    )


def pick(stacked, index, axis=0):
    return lax.dynamic_index_in_dim(stacked, index, axis, keepdims=False)


def halving_sum(blocks, axis_name):
    members = blocks.shape[1]
    size = lax.axis_size(axis_name)
    index = lax.axis_index(axis_name)
    bit = 1
    while bit < size:
        mine = (index // bit) % 2
        paired = blocks.reshape(blocks.shape[0], members // 2, 2, *blocks.shape[2:])
        away = pick(paired, 1 - mine, 2)
        arrived = lax.ppermute(away, axis_name, [(i, i ^ bit) for i in range(size)])
        blocks = pick(paired, mine, 2) + arrived
        members //= 2
        bit *= 2
    return blocks[:, 0]


def line_sum(blocks, axis_name):
    size = lax.axis_size(axis_name)
    index = lax.axis_index(axis_name)
    up, down = None, None
    for step in range(1, size):
        for_up = pick(blocks, jnp.minimum(index + size - step, size - 1))
        for_down = pick(blocks, jnp.maximum(index - size + step, 0))
        if up is not None:
            for_up = for_up + up
            for_down = for_down + down
        up = lax.ppermute(for_up, axis_name, [(i, i + 1) for i in range(step)])
        down = lax.ppermute(for_down, axis_name, [(i, i - 1) for i in range(size - step, size)])
    return pick(blocks, index) + up + down


def line_gather(block, axis_name):
    size = lax.axis_size(axis_name)
    index = lax.axis_index(axis_name)
    ups, downs = [block], [block]
    for _ in range(1, size):
        ups.append(lax.ppermute(ups[-1], axis_name, [(i, i + 1) for i in range(size - 1)]))
        downs.append(lax.ppermute(downs[-1], axis_name, [(i, i - 1) for i in range(1, size)]))
    relative = [block] + [
        jnp.where(index >= back, ups[back], downs[size - back]) for back in range(1, size)
    ]
    relative = jnp.stack(relative)
    return [pick(relative, (index - place + size) % size) for place in range(size)]


def reorder(positions, rows):
    chosen = (positions[:, None] == jnp.arange(rows.shape[0])[None, :]).astype(rows.dtype)
    return jnp.dot(chosen, rows, preferred_element_type=jnp.float32).astype(rows.dtype)


def shards(window, panels, row_map, panel_root, upper_blocks, diag_inverse, weights, pole_order):
    n_row, n_col, n_pole = (lax.axis_size(name) for name in ("row", "col", "pole"))
    row_index, col_index = lax.axis_index("row"), lax.axis_index("col")
    window_block = window[0]
    slab = panels[0, 0]
    width = slab.shape[1]
    group = window_block.shape[0] // n_row
    share = group // n_pole
    pole_weight = jnp.sum(jnp.where(jnp.arange(weights.shape[0]) == pole_order[0], weights, 0.0))
    shifts = [(col_index - panel_root[0, k] + n_col) % n_col for k in range(NS)]
    local_map = row_map.reshape(NS, n_col, group) % group

    slabs = [slab] + [
        lax.ppermute(slab, "col", [(i, (i + shift) % n_col) for i in range(n_col)])
        for shift in range(1, n_col)
    ]
    own_map = pick(local_map, col_index, 1).reshape(-1)
    packed_map = jnp.concatenate([own_map // 32, own_map % 32]).astype(jnp.bfloat16)
    pad = -packed_map.shape[0] % width
    packed_map = jnp.pad(packed_map, (0, pad)).reshape(-1, width)
    own_part = lax.dynamic_slice_in_dim(slab, col_index * group, group, 0)
    part_rows = upper_blocks.shape[2]
    first = jnp.concatenate([own_part, upper_blocks[0].reshape(-1, width), packed_map])
    gathered = line_gather(first, "row")
    others = [
        line_gather(lax.dynamic_slice_in_dim(other, col_index * group, group, 0), "row")
        for other in slabs[1:]
    ]
    pairs = upper_blocks.shape[1]
    factors = jnp.concatenate(
        [g[group : group + pairs * part_rows].reshape(pairs, part_rows, width) for g in gathered],
        axis=1,
    )
    maps = []
    for g in gathered:
        flat = g[group + pairs * part_rows :].reshape(-1)[: 2 * NS * group].astype(jnp.int32)
        maps.append((flat[: NS * group] * 32 + flat[NS * group :]).reshape(NS, group))

    stacked_slabs = jnp.stack(slabs)
    aligned = []
    for k in range(NS):
        rows = pick(stacked_slabs, shifts[k]).reshape(n_col, group, width)
        aligned.append(jnp.concatenate([reorder(local_map[k, c], rows[c]) for c in range(n_col)]))
    aligned = jnp.concatenate(aligned, axis=1)

    step = share // CHUNKS
    window_rows = window_block.reshape(n_row * n_pole, share, window_block.shape[1])
    column_parts, halves = [], []
    for chunk in range(CHUNKS):
        rows = window_rows[:, chunk * step : (chunk + 1) * step].reshape(-1, window_block.shape[1])
        y_window = jnp.dot(rows, aligned, preferred_element_type=jnp.float32) * (-pole_weight)
        columns, column_halves = [], []
        for k in range(NS):
            column = y_window[:, k * width : (k + 1) * width]
            for m in range(k):
                column = column - times_factor(column_halves[m], factors[pair_index(k, m)])
            columns.append(column)
            column_halves.append(split(column))
        halves.append(column_halves)
        terms = jnp.concatenate(columns, axis=1).reshape(n_row, n_pole, step, NS * width)
        column_parts.append(line_sum(halving_sum(terms, "pole"), "row"))
    summed_columns = jnp.concatenate(column_parts, axis=0).reshape(share, NS, width)
    summed_columns = summed_columns.transpose(1, 0, 2)

    inner = {}
    for k in range(NS):
        own = []
        for place in range(n_row):
            sources = jnp.stack(
                [gathered[place][:group]] + [other[place] for other in others]
            )
            own.append(reorder(maps[place][k], pick(sources, shifts[k])))
        own = jnp.concatenate(own).reshape(n_row * n_pole, share, width)
        for m in range(k + 1):
            total = 0.0
            for chunk in range(CHUNKS):
                own_chunk = own[:, chunk * step : (chunk + 1) * step].reshape(-1, width).T
                for half in halves[chunk][m]:
                    total = total + jnp.dot(own_chunk, half, preferred_element_type=jnp.float32)
            inner[k, m] = total

    wide = [factors[e].astype(jnp.float32) for e in range(pairs)]
    spread = jnp.zeros((NS, diag_inverse.shape[2] * n_row, width), jnp.float32)
    spread = lax.dynamic_update_slice_in_dim(
        spread, diag_inverse[0] * (pole_weight / n_col), row_index * diag_inverse.shape[2], 1
    )
    diagonals, crossed = [], {}

    def inverse_block(m, n):
        if m == n:
            return diagonals[m]
        return crossed[m, n] if m < n else crossed[n, m].T

    for k in range(NS):
        diagonal = spread[k] - inner[k, k]
        for m in range(k):
            y_block = inner[k, m].T
            for n in range(k):
                y_block = y_block + precise(inverse_block(m, n), wide[pair_index(k, n)])
            crossed[m, k] = -y_block
            diagonal = diagonal + precise(wide[pair_index(k, m)].T, y_block)
        diagonals.append(diagonal)
    terms = jnp.concatenate(diagonals, axis=1).reshape(n_row, n_pole, -1, NS * width)
    summed_diagonals = line_sum(halving_sum(terms, "pole"), "row")
    bit = 1
    while bit < n_col:
        summed_diagonals = summed_diagonals + lax.ppermute(
            summed_diagonals, "col", [(i, i ^ bit) for i in range(n_col)]
        )
        bit *= 2
    summed_diagonals = summed_diagonals.reshape(-1, NS, width).transpose(1, 0, 2)
    return (summed_columns[:, None], summed_diagonals)


def solution(mesh):
    return jax.shard_map(
        shards,
        mesh=mesh,
        in_specs=(
            P("pole", "col", "row"),
            P("pole", "col", "row", None),
            P(None, "row"),
            P("pole", None),
            P("pole", None, "row", None),
            P("pole", None, "row", None),
            P(),
            P("pole"),
        ),
        out_specs=(P(None, "col", ("row", "pole"), None), P(None, ("row", "pole"), None)),
        check_vma=False,
    )
```

```python
import jax
import jax.numpy as jnp
from jax import lax
from jax.experimental import pallas as pl
from jax.experimental.pallas import tpu as pltpu
from jax.sharding import PartitionSpec as P

NS = 3
CHUNKS = 2


def precise(left, right):
    return jnp.dot(left, right, precision=lax.Precision.HIGHEST, preferred_element_type=jnp.float32)


def pair_index(current, earlier):
    return current * (current - 1) // 2 + earlier


def split(value):
    high = value.astype(jnp.bfloat16)
    return high, (value - high.astype(jnp.float32)).astype(jnp.bfloat16)


def pick(stacked, index, axis=0):
    return lax.dynamic_index_in_dim(stacked, index, axis, keepdims=False)


def halving_step(halves, axis_name, bit):
    size = lax.axis_size(axis_name)
    mine, away = halves
    return mine, lax.ppermute(away, axis_name, [(i, i ^ bit) for i in range(size)])


def halving_sum(mine, away, axis_name):
    size = lax.axis_size(axis_name)
    index = lax.axis_index(axis_name)
    mine, arrived = halving_step((mine, away), axis_name, 1)
    bit = 2
    while bit < size:
        side = (index // bit) % 2
        shape = (mine.shape[0], mine.shape[1] // 2, 2) + mine.shape[2:]
        kept, come = mine.reshape(shape), arrived.reshape(shape)
        away = pick(kept, 1 - side, 2) + pick(come, 1 - side, 2)
        mine = pick(kept, side, 2) + pick(come, side, 2)
        mine, arrived = halving_step((mine, away), axis_name, bit)
        bit *= 2
    return (mine + arrived)[:, 0]


def line_sum(blocks, axis_name):
    size = lax.axis_size(axis_name)
    index = lax.axis_index(axis_name)
    up, down = None, None
    for step in range(1, size):
        for_up = pick(blocks, jnp.minimum(index + size - step, size - 1))
        for_down = pick(blocks, jnp.maximum(index - size + step, 0))
        if up is not None:
            for_up = for_up + up
            for_down = for_down + down
        up = lax.ppermute(for_up, axis_name, [(i, i + 1) for i in range(step)])
        down = lax.ppermute(for_down, axis_name, [(i, i - 1) for i in range(size - step, size)])
    return pick(blocks, index) + up + down


def line_gather(block, axis_name):
    size = lax.axis_size(axis_name)
    index = lax.axis_index(axis_name)
    ups, downs = [block], [block]
    for _ in range(1, size):
        ups.append(lax.ppermute(ups[-1], axis_name, [(i, i + 1) for i in range(size - 1)]))
        downs.append(lax.ppermute(downs[-1], axis_name, [(i, i - 1) for i in range(1, size)]))
    return [block] + [
        jnp.where(index >= back, ups[back], downs[size - back]) for back in range(1, size)
    ]


def reorder(positions, rows):
    chosen = (positions[:, None] == jnp.arange(rows.shape[0])[None, :]).astype(rows.dtype)
    return jnp.dot(chosen, rows, preferred_element_type=jnp.float32).astype(rows.dtype)


def window_kernel(core_ref, weight_ref, window_ref, aligned_ref, factor_ref, away_ref, keep_ref):
    width = factor_ref.shape[2]
    half = pl.num_programs(0) // 2
    y_window = jnp.dot(window_ref[0], aligned_ref[...], preferred_element_type=jnp.float32)
    y_window = y_window * weight_ref[0]
    columns, parts = [], []
    for k in range(NS):
        column = y_window[:, k * width : (k + 1) * width]
        for m in range(k):
            for part in parts[m]:
                column = column - jnp.dot(
                    part, factor_ref[pair_index(k, m)], preferred_element_type=jnp.float32
                )
        columns.append(column)
        parts.append(split(column))

    @pl.when(pl.program_id(0) < half)
    def _():
        for k in range(NS):
            away_ref[0, 0, :, k * width : (k + 1) * width] = columns[k]

    @pl.when(pl.program_id(0) >= half)
    def _():
        for k in range(NS):
            keep_ref[0, 0, :, k * width : (k + 1) * width] = columns[k]


def window_columns(core, scale, window_rows, aligned, factors, chunk, step, n_row, n_pole):
    blocks = n_row * n_pole
    half, side = blocks // 2, n_pole // 2
    depth, total = aligned.shape

    def window_at(i, core_ref):
        j = i % half
        core_now = jnp.where(i < half, 1 - core_ref[0], core_ref[0])
        return (j // side) * n_pole + (j % side) * 2 + core_now, chunk, 0

    def away_at(i, core_ref):
        j = jnp.minimum(i, half - 1)
        return j // side, j % side, 0, 0

    def keep_at(i, core_ref):
        j = jnp.maximum(i - half, 0)
        return j // side, j % side, 0, 0

    shape = jax.ShapeDtypeStruct((n_row, side, step, total), jnp.float32)
    return pl.pallas_call(
        window_kernel,
        out_shape=(shape, shape),
        grid_spec=pltpu.PrefetchScalarGridSpec(
            num_scalar_prefetch=1,
            grid=(blocks,),
            in_specs=[
                pl.BlockSpec(memory_space=pltpu.SMEM),
                pl.BlockSpec((1, step, depth), window_at),
                pl.BlockSpec((depth, total), lambda i, c: (0, 0)),
                pl.BlockSpec(factors.shape, lambda i, c: (0, 0, 0)),
            ],
            out_specs=(
                pl.BlockSpec((1, 1, step, total), away_at),
                pl.BlockSpec((1, 1, step, total), keep_at),
            ),
        ),
        cost_estimate=pl.CostEstimate(
            flops=2 * blocks * step * depth * total,
            bytes_accessed=2 * blocks * step * (depth + 2 * total),
            transcendentals=0,
        ),
    )(core, scale, window_rows, aligned, factors)


def inner_kernel(place_ref, own_away_ref, own_keep_ref, away_ref, keep_ref, sum_ref):
    width = sum_ref.shape[1]

    @pl.when((pl.program_id(0) == 0) & (pl.program_id(1) == 0))
    def _():
        sum_ref[...] = jnp.zeros_like(sum_ref)

    for own_ref, term_ref in ((own_away_ref, away_ref), (own_keep_ref, keep_ref)):
        for m in range(NS):
            for part in split(term_ref[0, 0, :, m * width : (m + 1) * width]):
                for k in range(m, NS):
                    sum_ref[k * (k + 1) // 2 + m] += lax.dot_general(
                        own_ref[0, 0, :, k * width : (k + 1) * width],
                        part,
                        (((0,), (0,)), ((), ())),
                        preferred_element_type=jnp.float32,
                    )


def inner_products(place, own, away, keep, chunk, step, width):
    n_row, side, _, total = away.shape
    n_pole = 2 * side

    def own_at(flip):
        def at(d, j, place_ref):
            core = 1 - place_ref[1] if flip else place_ref[1]
            return d, j * 2 + core, chunk, 0

        return at

    def term_at(d, j, place_ref):
        return (place_ref[0] - d + n_row) % n_row, j, 0, 0

    pairs = NS * (NS + 1) // 2
    return pl.pallas_call(
        inner_kernel,
        out_shape=jax.ShapeDtypeStruct((pairs, width, width), jnp.float32),
        grid_spec=pltpu.PrefetchScalarGridSpec(
            num_scalar_prefetch=1,
            grid=(n_row, side),
            in_specs=[
                pl.BlockSpec((1, 1, step, total), own_at(True)),
                pl.BlockSpec((1, 1, step, total), own_at(False)),
                pl.BlockSpec((1, 1, step, total), term_at),
                pl.BlockSpec((1, 1, step, total), term_at),
            ],
            out_specs=pl.BlockSpec((pairs, width, width), lambda d, j, p: (0, 0, 0)),
        ),
        cost_estimate=pl.CostEstimate(
            flops=4 * n_row * n_pole * step * pairs * width * width,
            bytes_accessed=6 * n_row * n_pole * step * total,
            transcendentals=0,
        ),
    )(place, own, own, away, keep)


def shards(window, panels, row_map, panel_root, upper_blocks, diag_inverse, weights, pole_order):
    n_row, n_col, n_pole = (lax.axis_size(name) for name in ("row", "col", "pole"))
    row_index, col_index = lax.axis_index("row"), lax.axis_index("col")
    window_block = window[0]
    slab = panels[0, 0]
    width = slab.shape[1]
    group = window_block.shape[0] // n_row
    share = group // n_pole
    pole_weight = jnp.sum(jnp.where(jnp.arange(weights.shape[0]) == pole_order[0], weights, 0.0))
    shifts = [(col_index - panel_root[0, k] + n_col) % n_col for k in range(NS)]
    core = lax.axis_index("pole") % 2
    local_map = row_map % group

    slabs = [slab] + [
        lax.ppermute(slab, "col", [(i, (i + shift) % n_col) for i in range(n_col)])
        for shift in range(1, n_col)
    ]
    own_map = lax.dynamic_slice_in_dim(local_map, col_index * group, group, 1)
    packed_map = jnp.concatenate([own_map // 32, own_map % 32]).astype(jnp.bfloat16).reshape(-1)
    packed_map = jnp.pad(packed_map, (0, -packed_map.shape[0] % width)).reshape(-1, width)
    part_rows = upper_blocks.shape[2]
    pairs = upper_blocks.shape[1]
    gathered = line_gather(
        jnp.concatenate([upper_blocks[0].reshape(-1, width), packed_map]), "row"
    )
    factors = jnp.zeros((pairs, part_rows * n_row, width), upper_blocks.dtype)
    maps = []
    for back, g in enumerate(gathered):
        place = (row_index - back + n_row) % n_row
        factors = lax.dynamic_update_slice_in_dim(
            factors, g[: pairs * part_rows].reshape(pairs, part_rows, width), place * part_rows, 1
        )
        flat = g[pairs * part_rows :].reshape(-1)[: 2 * NS * group].astype(jnp.int32)
        maps.append((flat[: NS * group] * 32 + flat[NS * group :]).reshape(NS, group))

    stacked_slabs = jnp.stack(slabs)
    stacked_own = lax.dynamic_slice_in_dim(stacked_slabs, col_index * group, group, 1)
    aligned = []
    for k in range(NS):
        rows = pick(stacked_slabs, shifts[k]).reshape(n_col, group, width)
        aligned.append(
            jnp.concatenate(
                [reorder(local_map[k, c * group : (c + 1) * group], rows[c]) for c in range(n_col)]
            )
        )
    aligned = jnp.concatenate(aligned, axis=1)

    step = share // CHUNKS if share % (8 * CHUNKS) == 0 else share
    chunks = share // step
    window_rows = window_block.reshape(n_row * n_pole, share, window_block.shape[1])
    core_ref = core.astype(jnp.int32).reshape(1)
    scale = (-pole_weight).reshape(1)
    terms = [
        window_columns(
            core_ref, scale, window_rows, aligned, factors, chunk, step, n_row, n_pole
        )
        for chunk in range(chunks)
    ]
    column_parts = [
        line_sum(halving_sum(keep, away, "pole"), "row") for away, keep in terms
    ]
    summed_columns = jnp.stack(
        [
            jnp.concatenate([part[:, k * width : (k + 1) * width] for part in column_parts])
            for k in range(NS)
        ]
    )

    sources = line_gather(stacked_own, "row")
    own = jnp.stack(
        [
            jnp.concatenate(
                [reorder(maps[d][k], pick(sources[d], shifts[k])) for k in range(NS)], axis=1
            ).reshape(n_pole, share, NS * width)
            for d in range(n_row)
        ]
    )
    place_ref = jnp.stack([row_index, core]).astype(jnp.int32)
    products = [
        inner_products(place_ref, own, away, keep, chunk, step, width)
        for chunk, (away, keep) in enumerate(terms)
    ]
    products = sum(products[1:], products[0])
    inner = {(k, m): products[k * (k + 1) // 2 + m] for k in range(NS) for m in range(k + 1)}

    wide = [factors[e].astype(jnp.float32) for e in range(pairs)]
    spread = jnp.zeros((NS, diag_inverse.shape[2] * n_row, width), jnp.float32)
    spread = lax.dynamic_update_slice_in_dim(
        spread, diag_inverse[0] * (pole_weight / n_col), row_index * diag_inverse.shape[2], 1
    )
    diagonals, crossed = [], {}

    def inverse_block(m, n):
        if m == n:
            return diagonals[m]
        return crossed[m, n] if m < n else crossed[n, m].T

    for k in range(NS):
        diagonal = spread[k] - inner[k, k]
        for m in range(k):
            y_block = inner[k, m].T
            for n in range(k):
                y_block = y_block + precise(inverse_block(m, n), wide[pair_index(k, n)])
            crossed[m, k] = -y_block
            diagonal = diagonal + precise(wide[pair_index(k, m)].T, y_block)
        diagonals.append(diagonal)
    blocks = jnp.concatenate(diagonals, axis=1).reshape(n_row, n_pole // 2, 2, -1, NS * width)
    summed_diagonals = line_sum(
        halving_sum(pick(blocks, core, 2), pick(blocks, 1 - core, 2), "pole"), "row"
    )
    bit = 1
    while bit < n_col:
        summed_diagonals = summed_diagonals + lax.ppermute(
            summed_diagonals, "col", [(i, i ^ bit) for i in range(n_col)]
        )
        bit *= 2
    summed_diagonals = summed_diagonals.reshape(-1, NS, width).transpose(1, 0, 2)
    return (summed_columns[:, None], summed_diagonals)


def solution(mesh):
    return jax.shard_map(
        shards,
        mesh=mesh,
        in_specs=(
            P("pole", "col", "row"),
            P("pole", "col", "row", None),
            P(None, "row"),
            P("pole", None),
            P("pole", None, "row", None),
            P("pole", None, "row", None),
            P(),
            P("pole"),
        ),
        out_specs=(P(None, "col", ("row", "pole"), None), P(None, ("row", "pole"), None)),
        check_vma=False,
    )
```

```python
import jax
import jax.numpy as jnp
from jax import lax
from jax.experimental import pallas as pl
from jax.experimental.pallas import tpu as pltpu
from jax.sharding import PartitionSpec as P

NS = 3
CHUNKS = 2


def precise(left, right):
    return jnp.dot(left, right, precision=lax.Precision.HIGHEST, preferred_element_type=jnp.float32)


def pair_index(current, earlier):
    return current * (current - 1) // 2 + earlier


def split(value):
    high = value.astype(jnp.bfloat16)
    return high, (value - high.astype(jnp.float32)).astype(jnp.bfloat16)


def pick(stacked, index, axis=0):
    return lax.dynamic_index_in_dim(stacked, index, axis, keepdims=False)


def swap(block, axis_name, bit):
    size = lax.axis_size(axis_name)
    return lax.ppermute(block, axis_name, [(i, i ^ bit) for i in range(size)])


def shift(block, axis_name, distance):
    size = lax.axis_size(axis_name)
    return lax.ppermute(block, axis_name, [(i, (i + distance) % size) for i in range(size)])


def halving_sum(blocks, axis_name, bit):
    size = lax.axis_size(axis_name)
    index = lax.axis_index(axis_name)
    while bit < size:
        side = (index // bit) % 2
        paired = blocks.reshape((blocks.shape[0], blocks.shape[1] // 2, 2) + blocks.shape[2:])
        blocks = pick(paired, side, 2) + swap(pick(paired, 1 - side, 2), axis_name, bit)
        bit *= 2
    return blocks[:, 0]


def shift_sum(blocks, axis_name):
    size = lax.axis_size(axis_name)
    index = lax.axis_index(axis_name)
    arrived = [
        shift(pick(blocks, (index + distance) % size), axis_name, distance)
        for distance in range(1, size)
    ]
    return sum(arrived, pick(blocks, index))


def shift_gather(block, axis_name):
    size = lax.axis_size(axis_name)
    return [block] + [shift(block, axis_name, distance) for distance in range(1, size)]


def reorder_kernel(slab_ref, map_ref, rows_ref, out_ref):
    size = rows_ref.shape[2]
    chosen = lax.broadcasted_iota(jnp.int32, (size, size), 0) == map_ref[0, 0]
    out_ref[...] = lax.dot_general(
        jnp.where(chosen, 1.0, 0.0).astype(rows_ref.dtype),
        rows_ref[0, 0],
        (((0,), (0,)), ((), ())),
        preferred_element_type=jnp.float32,
    ).astype(out_ref.dtype)


def reorder(slab_index, maps, sources):
    _, groups, group, width = sources.shape
    return pl.pallas_call(
        reorder_kernel,
        out_shape=jax.ShapeDtypeStruct((groups * group, NS * width), sources.dtype),
        grid_spec=pltpu.PrefetchScalarGridSpec(
            num_scalar_prefetch=1,
            grid=(groups, NS),
            in_specs=[
                pl.BlockSpec((1, 1, 1, group), lambda a, k, slabs: (a, k, 0, 0)),
                pl.BlockSpec((1, 1, group, width), lambda a, k, slabs: (slabs[k], a, 0, 0)),
            ],
            out_specs=pl.BlockSpec((group, width), lambda a, k, slabs: (a, k)),
        ),
        cost_estimate=pl.CostEstimate(
            flops=2 * groups * NS * group * group * width,
            bytes_accessed=4 * groups * NS * group * width,
            transcendentals=0,
        ),
    )(slab_index, maps[:, :, None], sources)


def window_kernel(core_ref, weight_ref, window_ref, aligned_ref, factor_ref, away_ref, keep_ref):
    width = factor_ref.shape[2]
    half = pl.num_programs(0) // 2
    y_window = jnp.dot(window_ref[0], aligned_ref[...], preferred_element_type=jnp.float32)
    y_window = y_window * weight_ref[0]
    columns, parts = [], []
    for k in range(NS):
        column = y_window[:, k * width : (k + 1) * width]
        for m in range(k):
            for part in parts[m]:
                column = column - jnp.dot(
                    part, factor_ref[pair_index(k, m)], preferred_element_type=jnp.float32
                )
        columns.append(column)
        parts.append(split(column))

    @pl.when(pl.program_id(0) < half)
    def _():
        for k in range(NS):
            away_ref[0, 0, :, k * width : (k + 1) * width] = columns[k]

    @pl.when(pl.program_id(0) >= half)
    def _():
        for k in range(NS):
            keep_ref[0, 0, :, k * width : (k + 1) * width] = columns[k]


def window_columns(place, scale, window_rows, aligned, factors, other, n_row, n_pole):
    share = window_rows.shape[1]
    side = n_pole // 4
    half = n_row * side
    depth, total = aligned.shape

    def window_at(i, place_ref):
        j = i % half
        core = jnp.where(i < half, 1 - place_ref[1], place_ref[1])
        second = 1 - place_ref[2] if other else place_ref[2]
        return (j // side) * n_pole + (j % side) * 4 + second * 2 + core, 0, 0

    def away_at(i, place_ref):
        j = jnp.minimum(i, half - 1)
        return j // side, j % side, 0, 0

    def keep_at(i, place_ref):
        j = jnp.maximum(i - half, 0)
        return j // side, j % side, 0, 0

    shape = jax.ShapeDtypeStruct((n_row, side, share, total), jnp.float32)
    return pl.pallas_call(
        window_kernel,
        out_shape=(shape, shape),
        grid_spec=pltpu.PrefetchScalarGridSpec(
            num_scalar_prefetch=1,
            grid=(2 * half,),
            in_specs=[
                pl.BlockSpec(memory_space=pltpu.SMEM),
                pl.BlockSpec((1, share, depth), window_at),
                pl.BlockSpec((depth, total), lambda i, c: (0, 0)),
                pl.BlockSpec(factors.shape, lambda i, c: (0, 0, 0)),
            ],
            out_specs=(
                pl.BlockSpec((1, 1, share, total), away_at),
                pl.BlockSpec((1, 1, share, total), keep_at),
            ),
        ),
        cost_estimate=pl.CostEstimate(
            flops=4 * half * share * depth * total,
            bytes_accessed=4 * half * share * (depth + 2 * total),
            transcendentals=0,
        ),
    )(place, scale, window_rows, aligned, factors)


def inner_kernel(place_ref, own_away_ref, own_keep_ref, away_ref, keep_ref, sum_ref):
    width = sum_ref.shape[1]

    @pl.when((pl.program_id(0) == 0) & (pl.program_id(1) == 0))
    def _():
        sum_ref[...] = jnp.zeros_like(sum_ref)

    for own_ref, term_ref in ((own_away_ref, away_ref), (own_keep_ref, keep_ref)):
        for m in range(NS):
            for part in split(term_ref[0, 0, :, m * width : (m + 1) * width]):
                for k in range(m, NS):
                    sum_ref[k * (k + 1) // 2 + m] += lax.dot_general(
                        own_ref[0, 0, :, k * width : (k + 1) * width],
                        part,
                        (((0,), (0,)), ((), ())),
                        preferred_element_type=jnp.float32,
                    )


def inner_products(place, own, away, keep, other, width):
    n_row, side, share, total = away.shape
    n_pole = 4 * side

    def own_at(flip):
        def at(d, j, place_ref):
            core = 1 - place_ref[1] if flip else place_ref[1]
            second = 1 - place_ref[2] if other else place_ref[2]
            return d, j * 4 + second * 2 + core, 0, 0

        return at

    def term_at(d, j, place_ref):
        return (place_ref[0] - d + n_row) % n_row, j, 0, 0

    pairs = NS * (NS + 1) // 2
    return pl.pallas_call(
        inner_kernel,
        out_shape=jax.ShapeDtypeStruct((pairs, width, width), jnp.float32),
        grid_spec=pltpu.PrefetchScalarGridSpec(
            num_scalar_prefetch=1,
            grid=(n_row, side),
            in_specs=[
                pl.BlockSpec((1, 1, share, total), own_at(True)),
                pl.BlockSpec((1, 1, share, total), own_at(False)),
                pl.BlockSpec((1, 1, share, total), term_at),
                pl.BlockSpec((1, 1, share, total), term_at),
            ],
            out_specs=pl.BlockSpec((pairs, width, width), lambda d, j, p: (0, 0, 0)),
        ),
        cost_estimate=pl.CostEstimate(
            flops=2 * n_row * n_pole * share * pairs * width * width,
            bytes_accessed=3 * n_row * n_pole * share * total,
            transcendentals=0,
        ),
    )(place, own, own, away, keep)


def shards(window, panels, row_map, panel_root, upper_blocks, diag_inverse, weights, pole_order):
    n_row, n_col, n_pole = (lax.axis_size(name) for name in ("row", "col", "pole"))
    row_index, col_index = lax.axis_index("row"), lax.axis_index("col")
    window_block = window[0]
    slab = panels[0, 0]
    width = slab.shape[1]
    group = window_block.shape[0] // n_row
    share = group // n_pole
    pole_weight = jnp.sum(jnp.where(jnp.arange(weights.shape[0]) == pole_order[0], weights, 0.0))
    pole_index = lax.axis_index("pole")
    core, second = pole_index % 2, (pole_index // 2) % 2
    place = jnp.stack([row_index, core, second]).astype(jnp.int32)
    slab_index = (col_index - panel_root[0] + n_col) % n_col
    local_map = row_map % group
    own_start = col_index * group

    slabs = [slab] + [shift(slab, "col", distance) for distance in range(1, n_col)]
    own_map = lax.dynamic_slice_in_dim(local_map, own_start, group, 1)
    packed_map = jnp.concatenate([own_map // 32, own_map % 32]).astype(jnp.bfloat16).reshape(-1)
    packed_map = jnp.pad(packed_map, (0, -packed_map.shape[0] % width)).reshape(-1, width)
    part_rows = upper_blocks.shape[2]
    pairs = upper_blocks.shape[1]
    gathered = shift_gather(
        jnp.concatenate([upper_blocks[0].reshape(-1, width), packed_map]), "row"
    )
    own_slab = [shift_gather(lax.dynamic_slice_in_dim(slab, own_start, group, 0), "row")]
    factors = jnp.zeros((pairs, part_rows * n_row, width), upper_blocks.dtype)
    maps = []
    for back, g in enumerate(gathered):
        at = (row_index - back + n_row) % n_row
        factors = lax.dynamic_update_slice_in_dim(
            factors, g[: pairs * part_rows].reshape(pairs, part_rows, width), at * part_rows, 1
        )
        flat = g[pairs * part_rows :].reshape(-1)[: 2 * NS * group].astype(jnp.int32)
        maps.append((flat[: NS * group] * 32 + flat[NS * group :]).reshape(NS, group))

    aligned = reorder(
        slab_index,
        jnp.stack([local_map[:, c * group : (c + 1) * group] for c in range(n_col)]),
        jnp.stack(slabs).reshape(n_col, n_col, group, width),
    )
    own_slab += [
        shift_gather(lax.dynamic_slice_in_dim(other, own_start, group, 0), "row")
        for other in slabs[1:]
    ]

    window_rows = window_block.reshape(n_row * n_pole, share, window_block.shape[1])
    scale = (-pole_weight).reshape(1)
    first_away, first_keep = window_columns(
        place, scale, window_rows, aligned, factors, True, n_row, n_pole
    )
    last_away, last_keep = window_columns(
        place, scale, window_rows, aligned, factors, False, n_row, n_pole
    )
    first_come = swap(first_away, "pole", 1)
    last_come = swap(last_away, "pole", 1)
    step = share // CHUNKS if share % (8 * CHUNKS) == 0 else share
    pieces = [slice(at, at + step) for at in range(0, share, step)]
    sent = [first_keep[:, :, piece] + first_come[:, :, piece] for piece in pieces]
    kept = [last_keep[:, :, piece] + last_come[:, :, piece] for piece in pieces]
    sent, own_slab = lax.optimization_barrier((sent, own_slab))
    column_parts = []
    for away, keep in zip(sent, kept):
        total = keep + swap(away, "pole", 2)
        column_parts.append(shift_sum(halving_sum(total, "pole", 4), "row"))
    summed_columns = jnp.stack(
        [
            jnp.concatenate([part[:, k * width : (k + 1) * width] for part in column_parts])
            for k in range(NS)
        ]
    )

    own = reorder(
        slab_index, jnp.stack(maps), jnp.stack([jnp.stack(blocks) for blocks in own_slab])
    ).reshape(n_row, n_pole, share, NS * width)
    products = inner_products(place, own, first_away, first_keep, True, width) + inner_products(
        place, own, last_away, last_keep, False, width
    )
    inner = {(k, m): products[k * (k + 1) // 2 + m] for k in range(NS) for m in range(k + 1)}

    wide = [factors[e].astype(jnp.float32) for e in range(pairs)]
    spread = jnp.zeros((NS, diag_inverse.shape[2] * n_row, width), jnp.float32)
    spread = lax.dynamic_update_slice_in_dim(
        spread, diag_inverse[0] * (pole_weight / n_col), row_index * diag_inverse.shape[2], 1
    )
    diagonals, crossed = [], {}

    def inverse_block(m, n):
        if m == n:
            return diagonals[m]
        return crossed[m, n] if m < n else crossed[n, m].T

    for k in range(NS):
        diagonal = spread[k] - inner[k, k]
        for m in range(k):
            y_block = inner[k, m].T
            for n in range(k):
                y_block = y_block + precise(inverse_block(m, n), wide[pair_index(k, n)])
            crossed[m, k] = -y_block
            diagonal = diagonal + precise(wide[pair_index(k, m)].T, y_block)
        diagonals.append(diagonal)
    blocks = jnp.concatenate(diagonals, axis=1).reshape(n_row, n_pole, -1, NS * width)
    summed_diagonals = shift_sum(halving_sum(blocks, "pole", 1), "row")
    bit = 1
    while bit < n_col:
        summed_diagonals = summed_diagonals + lax.ppermute(
            summed_diagonals, "col", [(i, i ^ bit) for i in range(n_col)]
        )
        bit *= 2
    summed_diagonals = summed_diagonals.reshape(-1, NS, width).transpose(1, 0, 2)
    return (summed_columns[:, None], summed_diagonals)


def solution(mesh):
    return jax.shard_map(
        shards,
        mesh=mesh,
        in_specs=(
            P("pole", "col", "row"),
            P("pole", "col", "row", None),
            P(None, "row"),
            P("pole", None),
            P("pole", None, "row", None),
            P("pole", None, "row", None),
            P(),
            P("pole"),
        ),
        out_specs=(P(None, "col", ("row", "pole"), None), P(None, ("row", "pole"), None)),
        check_vma=False,
    )
```

```python
import jax
import jax.numpy as jnp
from jax import lax
from jax.experimental import pallas as pl
from jax.experimental.pallas import tpu as pltpu
from jax.sharding import PartitionSpec as P


NS = 3
CHUNKS = 2


def precise(left, right):
    return jnp.dot(left, right, precision=lax.Precision.HIGHEST, preferred_element_type=jnp.float32)


def pair_index(current, earlier):
    return current * (current - 1) // 2 + earlier


def split(value):
    high = value.astype(jnp.bfloat16)
    return high, (value - high.astype(jnp.float32)).astype(jnp.bfloat16)


def pick(stacked, index, axis=0):
    return lax.dynamic_index_in_dim(stacked, index, axis, keepdims=False)


def swap(block, axis_name, bit):
    size = lax.axis_size(axis_name)
    return lax.ppermute(block, axis_name, [(i, i ^ bit) for i in range(size)])


def shift(block, axis_name, distance):
    size = lax.axis_size(axis_name)
    return lax.ppermute(block, axis_name, [(i, (i + distance) % size) for i in range(size)])


def halving_sum(blocks, axis_name, bit):
    size = lax.axis_size(axis_name)
    index = lax.axis_index(axis_name)
    while bit < size:
        side = (index // bit) % 2
        paired = blocks.reshape((blocks.shape[0], blocks.shape[1] // 2, 2) + blocks.shape[2:])
        blocks = pick(paired, side, 2) + swap(pick(paired, 1 - side, 2), axis_name, bit)
        bit *= 2
    return blocks[:, 0]


def shift_sum(blocks, axis_name):
    size = lax.axis_size(axis_name)
    index = lax.axis_index(axis_name)
    total = pick(blocks, index)
    arrived = []
    for distance in range(1, size):
        arrived.append(shift(pick(blocks, (index + distance) % size), axis_name, distance))
    return sum(arrived, total)


def shift_gather(block, axis_name):
    size = lax.axis_size(axis_name)
    blocks = [block]
    for distance in range(1, size):
        blocks.append(shift(block, axis_name, distance))
    return blocks


def reorder_kernel(slab_ref, map_ref, rows_ref, out_ref):
    size = rows_ref.shape[2]
    chosen = lax.broadcasted_iota(jnp.int32, (size, size), 0) == map_ref[0, 0]
    out_ref[...] = lax.dot_general(
        jnp.where(chosen, 1.0, 0.0).astype(rows_ref.dtype),
        rows_ref[0, 0],
        (((0,), (0,)), ((), ())),
        preferred_element_type=jnp.float32,
    ).astype(out_ref.dtype)


def reorder(slab_index, maps, sources):
    _, groups, group, width = sources.shape
    return pl.pallas_call(
        reorder_kernel,
        out_shape=jax.ShapeDtypeStruct((groups * group, NS * width), sources.dtype),
        grid_spec=pltpu.PrefetchScalarGridSpec(
            num_scalar_prefetch=1,
            grid=(groups, NS),
            in_specs=[
                pl.BlockSpec((1, 1, 1, group), lambda a, k, slabs: (a, k, 0, 0)),
                pl.BlockSpec((1, 1, group, width), lambda a, k, slabs: (slabs[k], a, 0, 0)),
            ],
            out_specs=pl.BlockSpec((group, width), lambda a, k, slabs: (a, k)),
        ),
        cost_estimate=pl.CostEstimate(
            flops=2 * groups * NS * group * group * width,
            bytes_accessed=4 * groups * NS * group * width,
            transcendentals=0,
        ),
    )(slab_index, maps[:, :, None], sources)


def window_kernel(core_ref, weight_ref, window_ref, aligned_ref, factor_ref, away_ref, keep_ref):
    width = factor_ref.shape[2]
    half = pl.num_programs(0) // 2
    y_window = jnp.dot(window_ref[0], aligned_ref[...], preferred_element_type=jnp.float32)
    y_window = y_window * weight_ref[0]
    columns, parts = [], []
    for k in range(NS):
        column = y_window[:, k * width : (k + 1) * width]
        for m in range(k):
            for part in parts[m]:
                column = column - jnp.dot(
                    part, factor_ref[pair_index(k, m)], preferred_element_type=jnp.float32
                )
        columns.append(column)
        parts.append(split(column))

    @pl.when(pl.program_id(0) < half)
    def _():
        for k in range(NS):
            away_ref[0, 0, :, k * width : (k + 1) * width] = columns[k]

    @pl.when(pl.program_id(0) >= half)
    def _():
        for k in range(NS):
            keep_ref[0, 0, :, k * width : (k + 1) * width] = columns[k]


def window_columns(place, scale, window_rows, aligned, factors, other, n_row, n_pole):
    share = window_rows.shape[1]
    side = n_pole // 4
    half = n_row * side
    depth, total = aligned.shape

    def window_at(i, place_ref):
        j = i % half
        core = jnp.where(i < half, 1 - place_ref[1], place_ref[1])
        second = 1 - place_ref[2] if other else place_ref[2]
        return (j // side) * n_pole + (j % side) * 4 + second * 2 + core, 0, 0

    def away_at(i, place_ref):
        j = jnp.minimum(i, half - 1)
        return j // side, j % side, 0, 0

    def keep_at(i, place_ref):
        j = jnp.maximum(i - half, 0)
        return j // side, j % side, 0, 0

    shape = jax.ShapeDtypeStruct((n_row, side, share, total), jnp.float32)
    return pl.pallas_call(
        window_kernel,
        out_shape=(shape, shape),
        grid_spec=pltpu.PrefetchScalarGridSpec(
            num_scalar_prefetch=1,
            grid=(2 * half,),
            in_specs=[
                pl.BlockSpec(memory_space=pltpu.SMEM),
                pl.BlockSpec((1, share, depth), window_at),
                pl.BlockSpec((depth, total), lambda i, c: (0, 0)),
                pl.BlockSpec(factors.shape, lambda i, c: (0, 0, 0)),
            ],
            out_specs=(
                pl.BlockSpec((1, 1, share, total), away_at),
                pl.BlockSpec((1, 1, share, total), keep_at),
            ),
        ),
        cost_estimate=pl.CostEstimate(
            flops=4 * half * share * depth * total,
            bytes_accessed=4 * half * share * (depth + 2 * total),
            transcendentals=0,
        ),
    )(place, scale, window_rows, aligned, factors)


def inner_kernel(place_ref, own_away_ref, own_keep_ref, away_ref, keep_ref, sum_ref):
    width = sum_ref.shape[1]

    @pl.when((pl.program_id(0) == 0) & (pl.program_id(1) == 0))
    def _():
        sum_ref[...] = jnp.zeros_like(sum_ref)

    for own_ref, term_ref in ((own_away_ref, away_ref), (own_keep_ref, keep_ref)):
        for m in range(NS):
            for part in split(term_ref[0, 0, :, m * width : (m + 1) * width]):
                for k in range(m, NS):
                    sum_ref[k * (k + 1) // 2 + m] += lax.dot_general(
                        own_ref[0, 0, :, k * width : (k + 1) * width],
                        part,
                        (((0,), (0,)), ((), ())),
                        preferred_element_type=jnp.float32,
                    )


def inner_products(place, own, away, keep, other, width):
    n_row, side, share, total = away.shape
    n_pole = 4 * side

    def own_at(flip):
        def at(d, j, place_ref):
            core = 1 - place_ref[1] if flip else place_ref[1]
            second = 1 - place_ref[2] if other else place_ref[2]
            return d, j * 4 + second * 2 + core, 0, 0

        return at

    def term_at(d, j, place_ref):
        return (place_ref[0] - d + n_row) % n_row, j, 0, 0

    pairs = NS * (NS + 1) // 2
    return pl.pallas_call(
        inner_kernel,
        out_shape=jax.ShapeDtypeStruct((pairs, width, width), jnp.float32),
        grid_spec=pltpu.PrefetchScalarGridSpec(
            num_scalar_prefetch=1,
            grid=(n_row, side),
            in_specs=[
                pl.BlockSpec((1, 1, share, total), own_at(True)),
                pl.BlockSpec((1, 1, share, total), own_at(False)),
                pl.BlockSpec((1, 1, share, total), term_at),
                pl.BlockSpec((1, 1, share, total), term_at),
            ],
            out_specs=pl.BlockSpec((pairs, width, width), lambda d, j, p: (0, 0, 0)),
        ),
        cost_estimate=pl.CostEstimate(
            flops=2 * n_row * n_pole * share * pairs * width * width,
            bytes_accessed=3 * n_row * n_pole * share * total,
            transcendentals=0,
        ),
    )(place, own, own, away, keep)


def staged(window, panels, row_map, panel_root, upper_blocks, diag_inverse, weights, pole_order):
    n_row, n_col, n_pole = (lax.axis_size(name) for name in ("row", "col", "pole"))
    row_index, col_index = lax.axis_index("row"), lax.axis_index("col")
    window_block = window[0]
    slab = panels[0, 0]
    width = slab.shape[1]
    group = window_block.shape[0] // n_row
    share = group // n_pole
    pole_weight = jnp.sum(jnp.where(jnp.arange(weights.shape[0]) == pole_order[0], weights, 0.0))
    pole_index = lax.axis_index("pole")
    core, second = pole_index % 2, (pole_index // 2) % 2
    place = jnp.stack([row_index, core, second]).astype(jnp.int32)
    slab_index = (col_index - panel_root[0] + n_col) % n_col
    local_map = row_map % group
    own_start = col_index * group

    slabs = [slab] + [shift(slab, "col", distance) for distance in range(1, n_col)]
    own_map = lax.dynamic_slice_in_dim(local_map, own_start, group, 1)
    packed_map = jnp.concatenate([own_map // 32, own_map % 32]).astype(jnp.bfloat16).reshape(-1)
    packed_map = jnp.pad(packed_map, (0, -packed_map.shape[0] % width)).reshape(-1, width)
    part_rows = upper_blocks.shape[2]
    pairs = upper_blocks.shape[1]
    gathered = shift_gather(
        jnp.concatenate([upper_blocks[0].reshape(-1, width), packed_map]), "row"
    )
    own_slab = [shift_gather(lax.dynamic_slice_in_dim(slab, own_start, group, 0), "row")]
    factors = jnp.zeros((pairs, part_rows * n_row, width), upper_blocks.dtype)
    maps = []
    for back, g in enumerate(gathered):
        at = (row_index - back + n_row) % n_row
        factors = lax.dynamic_update_slice_in_dim(
            factors, g[: pairs * part_rows].reshape(pairs, part_rows, width), at * part_rows, 1
        )
        flat = g[pairs * part_rows :].reshape(-1)[: 2 * NS * group].astype(jnp.int32)
        maps.append((flat[: NS * group] * 32 + flat[NS * group :]).reshape(NS, group))

    stacked_slabs = jnp.stack(slabs).reshape(n_col, n_col, group, width)
    stacked_map = jnp.stack([local_map[:, c * group : (c + 1) * group] for c in range(n_col)])
    aligned = reorder(slab_index, stacked_map, stacked_slabs)
    own_slab += [
        shift_gather(lax.dynamic_slice_in_dim(other, own_start, group, 0), "row")
        for other in slabs[1:]
    ]

    window_rows = window_block.reshape(n_row * n_pole, share, window_block.shape[1])
    scale = (-pole_weight).reshape(1)
    first_away, first_keep = window_columns(
        place, scale, window_rows, aligned, factors, True, n_row, n_pole
    )
    last_away, last_keep = window_columns(
        place, scale, window_rows, aligned, factors, False, n_row, n_pole
    )
    first_come = swap(first_away, "pole", 1)
    last_come = swap(last_away, "pole", 1)
    step = share // CHUNKS if share % (8 * CHUNKS) == 0 else share
    pieces = [slice(at, at + step) for at in range(0, share, step)]
    sent = [first_keep[:, :, piece] + first_come[:, :, piece] for piece in pieces]
    kept = [last_keep[:, :, piece] + last_come[:, :, piece] for piece in pieces]
    _, own_slab = lax.optimization_barrier((sent, own_slab))
    column_parts = []
    for away, keep in zip(sent, kept):
        arrived = swap(away, "pole", 2)
        total = keep + arrived
        column_parts.append(shift_sum(halving_sum(total, "pole", 4), "row"))
    summed_columns = jnp.stack(
        [
            jnp.concatenate([part[:, k * width : (k + 1) * width] for part in column_parts])
            for k in range(NS)
        ]
    )

    stacked_own = jnp.stack([jnp.stack(blocks) for blocks in own_slab])
    own = reorder(slab_index, jnp.stack(maps), stacked_own)
    own = own.reshape(n_row, n_pole, share, NS * width)
    products = inner_products(place, own, first_away, first_keep, True, width)
    products += inner_products(place, own, last_away, last_keep, False, width)
    inner = {(k, m): products[k * (k + 1) // 2 + m] for k in range(NS) for m in range(k + 1)}

    wide = [factors[e].astype(jnp.float32) for e in range(pairs)]
    spread = jnp.zeros((NS, diag_inverse.shape[2] * n_row, width), jnp.float32)
    spread = lax.dynamic_update_slice_in_dim(
        spread, diag_inverse[0] * (pole_weight / n_col), row_index * diag_inverse.shape[2], 1
    )
    diagonals, crossed = [], {}

    def inverse_block(m, n):
        if m == n:
            return diagonals[m]
        return crossed[m, n] if m < n else crossed[n, m].T

    for k in range(NS):
        diagonal = spread[k] - inner[k, k]
        for m in range(k):
            y_block = inner[k, m].T
            for n in range(k):
                y_block = y_block + precise(inverse_block(m, n), wide[pair_index(k, n)])
            crossed[m, k] = -y_block
            diagonal = diagonal + precise(wide[pair_index(k, m)].T, y_block)
        diagonals.append(diagonal)
    blocks = jnp.concatenate(diagonals, axis=1).reshape(n_row, n_pole, -1, NS * width)
    summed_diagonals = shift_sum(halving_sum(blocks, "pole", 1), "row")
    bit = 1
    while bit < n_col:
        summed_diagonals = summed_diagonals + lax.ppermute(
            summed_diagonals, "col", [(i, i ^ bit) for i in range(n_col)]
        )
        bit *= 2
    summed_diagonals = summed_diagonals.reshape(-1, NS, width).transpose(1, 0, 2)
    return (summed_columns[:, None], summed_diagonals)


def solution(mesh):
    return jax.shard_map(
        staged,
        mesh=mesh,
        in_specs=(
            P("pole", "col", "row"),
            P("pole", "col", "row", None),
            P(None, "row"),
            P("pole", None),
            P("pole", None, "row", None),
            P("pole", None, "row", None),
            P(),
            P("pole"),
        ),
        out_specs=(P(None, "col", ("row", "pole"), None), P(None, ("row", "pole"), None)),
        check_vma=False,
    )
```
